32 devices in a mesh: dp: 8 (over z, y), group: 4 (over x, core).
Axes of the slice: x: 2, y: 2, z: 4, core: 2. Of those that a mesh axis runs over, the one named last changes fastest.
Arguments:
- query_feats: bfloat16 [4096, 4096], P(('dp', 'group')), may hold values from -45 to 45
- passage_feats: bfloat16 [4096, 4096], P(('dp', 'group')), may hold values from -45 to 45
- head: bfloat16 [4096, 1024], replicated, may hold values from -0.09375 to 0.09375
- neg_ids: int32 [4096, 7], P(('dp', 'group')), may hold values from 0 to 4095, as said below
Outputs:
- head_grad: float32 [4096, 1024], P(('dp', 'group'))
- query_loss: float32 [4096], P(('dp', 'group'))
The draws below stay inside these ranges and needn't reach their ends.
Inputs may be any that keep to these rules, and one draw needn't show every extreme that they name: `neg_ids`: the 7 ids of a query name rows on 7 different devices, each with the query's group index and another dp index. Of the ids of one device's rows, at most 128 name rows of any one other device, and for every device some other device is named exactly 128 times.
All inputs are finite; a program needn't handle non-finite values.
Results may differ from the reference program's by a relative error of at most 0.0045.
The reference program's roundings to bfloat16 on the way count: a program that leaves them out, or rounds other values in their place, can miss the bound.
Values may be sent and summed in bfloat16 or wider, within the bound.
A program may use at most 128 MiB of HBM per device.

```python
import jax
import jax.numpy as jnp
from jax import lax

D = 4096
E = 1024
NEG = 7
TOK_DEV = 128
TOKENS = 4096
N_DP = 8
N_GROUP = 4


def feature_draw(key, salt):
    own_key = jax.random.fold_in(key, salt)
    key_noise, key_row, key_col = jax.random.split(own_key, 3)
    dev_total = N_DP * N_GROUP
    row_index = jnp.arange(TOKENS)
    device_pos = (row_index // TOK_DEV).astype(jnp.float32) / max(dev_total - 1, 1)
    rise = jnp.exp(jnp.log(3.0) * device_pos)[:, None]
    noise = jax.random.truncated_normal(key_noise, -4.0, 4.0, (TOKENS, D), jnp.float32)
    row_spread = jnp.exp(jax.random.uniform(key_row, (TOKENS, 1), jnp.float32, 0.0, jnp.log(10.0 / 3.0)))
    col_spread = jnp.exp(jax.random.uniform(key_col, (1, D), jnp.float32, 0.0, jnp.log(10.0)))
    return (noise * rise * row_spread * col_spread / 10.0).astype(jnp.bfloat16)


def draw_query_feats(key, part):
    return feature_draw(key, 11)


def draw_passage_feats(key, part):
    return feature_draw(key, 23)


def draw_neg_ids(key, part):
    dev_total = N_DP * N_GROUP
    other_count = N_DP - 1
    slot_total = NEG * TOK_DEV
    base_load = slot_total // other_count
    remainder = slot_total % other_count
    spread = max(0, min(base_load, TOK_DEV - base_load - 1))
    pair_count = (other_count - 2) // 2

    def one_device(device):
        dev_key = jax.random.fold_in(jax.random.fold_in(key, 37), device)
        key_pairs, key_amount, key_offset, key_local, key_order = jax.random.split(dev_key, 5)
        counts = base_load + (jnp.arange(other_count) < remainder).astype(jnp.int32)
        inner = jax.random.permutation(key_pairs, other_count - 2) + 1
        plus_side = inner[:pair_count]
        minus_side = inner[pair_count:2 * pair_count]
        amount = jax.random.randint(key_amount, (pair_count,), 0, spread + 1)
        counts = counts.at[plus_side].add(amount).at[minus_side].add(-amount)
        counts = counts.at[0].add(spread).at[other_count - 1].add(-spread)
        cumulative = jnp.cumsum(counts)
        slot_pos = jnp.arange(slot_total)
        owner_pos = jnp.sum((slot_pos[:, None] >= cumulative[None, :]).astype(jnp.int32), axis=1)
        offsets = 1 + jax.random.permutation(key_offset, other_count)[owner_pos]
        own_dp = device // N_GROUP
        own_group = device % N_GROUP
        owner_dp = (own_dp + offsets) % N_DP
        local_row = jax.random.randint(key_local, (slot_total,), 0, TOK_DEV)
        global_ids = (owner_dp * N_GROUP + own_group) * TOK_DEV + local_row
        table = global_ids.reshape(NEG, TOK_DEV).T
        order = jax.random.permutation(key_order, TOK_DEV)
        return table[order].astype(jnp.int32)
    return jax.vmap(one_device)(jnp.arange(dev_total)).reshape(TOKENS, NEG)


def bell_draw(rng, dims, scale, most, held_as=jnp.bfloat16):
    return jnp.clip(scale * jax.random.normal(rng, dims, jnp.float32), -most, most).astype(held_as)


def setup_inputs(seed: int = 0) -> dict:
    key_list = jax.random.split(jax.random.key(seed), 5)
    query_feats = draw_query_feats(jax.random.fold_in(key_list[4], 71), 0)
    passage_feats = draw_passage_feats(jax.random.fold_in(key_list[4], 71), 0)
    head = bell_draw(key_list[2], (D, E), D ** -0.5, 0.09375)
    neg_ids = draw_neg_ids(jax.random.fold_in(key_list[4], 71), 0)
    return dict(query_feats=query_feats, passage_feats=passage_feats, head=head, neg_ids=neg_ids)


scaling_divisor = 0.05
levels = 15.0
epsilon = 1e-06

def quantize(projected, low_bound, high_bound):
    as_float = projected.astype(jnp.float32)
    step_size = (high_bound - low_bound) / levels
    level_pos = (as_float - low_bound) / step_size
    quantized = low_bound + step_size * (level_pos - jnp.sin(2.0 * jnp.pi * level_pos) / (2.0 * jnp.pi))
    inverse = lax.rsqrt(lax.optimization_barrier(jnp.sum(quantized * quantized, axis=-1, keepdims=True)) + epsilon)
    return ((quantized * inverse).astype(jnp.bfloat16), quantized, inverse)

def norm_back(cotangent, quantized, inverse):
    inner_prod = lax.optimization_barrier(jnp.sum(quantized * cotangent, axis=-1, keepdims=True))
    return (inverse * cotangent - quantized * inverse ** 3 * inner_prod).astype(jnp.bfloat16)

def block_loss(anchor_vector_entries, inbatch_vector_entries, difficult_distractor_vectors, pos_mask):
    pairwise_cosine_scores = jnp.dot(anchor_vector_entries, inbatch_vector_entries.T, preferred_element_type=jnp.float32) / scaling_divisor
    difficult_distractor_scores = jnp.einsum('pgu,pu->pg', difficult_distractor_vectors.astype(jnp.float32), anchor_vector_entries.astype(jnp.float32)) / scaling_divisor
    positive = lax.optimization_barrier(jnp.sum(pairwise_cosine_scores * pos_mask, axis=1))
    exp_batch = jnp.exp(pairwise_cosine_scores)
    batch_total = lax.optimization_barrier(jnp.sum(exp_batch, axis=1))
    exp_pos = jnp.exp(positive)
    hard_exp = jnp.exp(difficult_distractor_scores)
    hard_total = exp_pos + lax.optimization_barrier(jnp.sum(hard_exp, axis=1))
    query_loss = jnp.log(batch_total) - positive + jnp.log(hard_total) - positive
    inbatch_normalized_share = (exp_batch / batch_total[:, None] - pos_mask * (2.0 - exp_pos / hard_total)[:, None]).astype(jnp.bfloat16)
    difficult_normalized_share = (hard_exp / hard_total[:, None]).astype(jnp.bfloat16)
    anchor_vector_derivative = (jnp.dot(inbatch_normalized_share, inbatch_vector_entries, preferred_element_type=jnp.float32) + jnp.einsum('mz,mzh->mh', difficult_normalized_share.astype(jnp.float32), difficult_distractor_vectors.astype(jnp.float32))) / scaling_divisor
    inbatch_vector_derivative = lax.dot_general(inbatch_normalized_share, anchor_vector_entries, (((0,), (0,)), ((), ())), preferred_element_type=jnp.float32) / scaling_divisor
    difficult_distractor_derivative = (difficult_normalized_share.astype(jnp.float32)[:, :, None] * anchor_vector_entries.astype(jnp.float32)[:, None, :] / scaling_divisor).astype(jnp.bfloat16)
    return (query_loss, anchor_vector_derivative, inbatch_vector_derivative, difficult_distractor_derivative)

def reference(query_feats, passage_feats, head, neg_ids):
    proj_query = jnp.dot(query_feats, head, preferred_element_type=jnp.float32).astype(jnp.bfloat16)
    proj_pass = jnp.dot(passage_feats, head, preferred_element_type=jnp.float32).astype(jnp.bfloat16)
    high_bound = jnp.maximum(lax.optimization_barrier(jnp.max(proj_query, axis=0)), lax.optimization_barrier(jnp.max(proj_pass, axis=0))).astype(jnp.float32)
    low_bound = jnp.minimum(lax.optimization_barrier(jnp.min(proj_query, axis=0)), lax.optimization_barrier(jnp.min(proj_pass, axis=0))).astype(jnp.float32)
    anchor_vector_entries, quant_query, inv_query = quantize(proj_query, low_bound, high_bound)
    pass_emb, quant_pass, inv_pass = quantize(proj_pass, low_bound, high_bound)
    difficult_distractor_vectors = pass_emb[neg_ids]
    cand_count = N_GROUP * TOK_DEV
    pos_mask = jnp.eye(cand_count, dtype=jnp.float32)
    query_blocks = anchor_vector_entries.reshape(N_DP, cand_count, E)
    pass_blocks = pass_emb.reshape(N_DP, cand_count, E)
    hard_blocks = difficult_distractor_vectors.reshape(N_DP, cand_count, NEG, E)

    def one_block(inputs):
        return block_loss(inputs[0], inputs[1], inputs[2], pos_mask)
    losses, query_grads, batch_grads, hard_grads = lax.map(one_block, (query_blocks, pass_blocks, hard_blocks))
    query_loss = losses.reshape(TOKENS)
    anchor_vector_derivative = query_grads.reshape(TOKENS, E)
    hard_flat = hard_grads.reshape(TOKENS * NEG, E).astype(jnp.float32)
    pass_grad = batch_grads.reshape(TOKENS, E) + jax.ops.segment_sum(hard_flat, neg_ids.reshape(-1).astype(jnp.int32), num_segments=TOKENS)
    proj_query_grad = norm_back(anchor_vector_derivative, quant_query, inv_query)
    proj_pass_grad = norm_back(pass_grad, quant_pass, inv_pass)
    head_grad = jnp.dot(query_feats.T, proj_query_grad, preferred_element_type=jnp.float32) + jnp.dot(passage_feats.T, proj_pass_grad, preferred_element_type=jnp.float32)
    return (head_grad, query_loss)
```

```python
import functools

import jax
import jax.numpy as jnp
from jax import lax
from jax.experimental import pallas as pl
from jax.experimental.pallas import tpu as pltpu
from jax.sharding import PartitionSpec as P

scaling_divisor = 0.05
levels = 15.0
epsilon = 1e-06
MESH = pl.DeviceIdType.MESH
VMEM = pl.BlockSpec(memory_space=pltpu.VMEM)


def quantize(projected, low_bound, high_bound):
    as_float = projected.astype(jnp.float32)
    step_size = (high_bound - low_bound) / levels
    level_pos = (as_float - low_bound) / step_size
    quantized = low_bound + step_size * (
        level_pos - jnp.sin(2.0 * jnp.pi * level_pos) / (2.0 * jnp.pi)
    )
    inverse = lax.rsqrt(jnp.sum(quantized * quantized, axis=-1, keepdims=True) + epsilon)
    return ((quantized * inverse).astype(jnp.bfloat16), quantized, inverse)


def norm_back(cotangent, quantized, inverse):
    inner_prod = jnp.sum(quantized * cotangent, axis=-1, keepdims=True)
    return (inverse * cotangent - quantized * inverse**3 * inner_prod).astype(jnp.bfloat16)


def bounds_kernel(n_dp, n_group, own, out, from_group, from_dp, mid, send_g, recv_g, send_d, recv_d):
    me_d, me_g = lax.axis_index("dp"), lax.axis_index("group")

    def exchange(src, landing, send, recv, count, target):
        copies = []
        for k in range(1, count):
            copy = pltpu.make_async_remote_copy(
                src_ref=src,
                dst_ref=landing.at[k],
                send_sem=send.at[k],
                recv_sem=recv.at[k],
                device_id=target(k),
                device_id_type=MESH,
            )
            copy.start()
            copies.append(copy)
        for copy in copies:
            copy.wait()
        total = src[...]
        for k in range(1, count):
            total = jnp.maximum(total, landing[k])
        return total

    mid[...] = exchange(
        own, from_group, send_g, recv_g, n_group, lambda k: (me_d, lax.rem(me_g + k, n_group))
    )
    out[...] = exchange(
        mid, from_dp, send_d, recv_d, n_dp, lambda k: (lax.rem(me_d + k, n_dp), me_g)
    )


def all_bounds(own, n_dp, n_group):
    return pl.pallas_call(
        functools.partial(bounds_kernel, n_dp, n_group),
        out_shape=jax.ShapeDtypeStruct(own.shape, own.dtype),
        in_specs=[VMEM],
        out_specs=VMEM,
        scratch_shapes=[
            pltpu.VMEM((n_group,) + own.shape, own.dtype),
            pltpu.VMEM((n_dp,) + own.shape, own.dtype),
            pltpu.VMEM(own.shape, own.dtype),
            pltpu.SemaphoreType.DMA((n_group,)),
            pltpu.SemaphoreType.DMA((n_group,)),
            pltpu.SemaphoreType.DMA((n_dp,)),
            pltpu.SemaphoreType.DMA((n_dp,)),
        ],
        compiler_params=pltpu.CompilerParams(has_side_effects=True),
        name="bounds",
    )(own)


def dot_nt(a, b):
    return lax.dot_general(a, b, (((1,), (1,)), ((), ())), preferred_element_type=jnp.float32)


def dot_tn(a, b):
    return lax.dot_general(a, b, (((0,), (0,)), ((), ())), preferred_element_type=jnp.float32)


def body(query_feats, passage_feats, head, neg_ids):
    rows, width = query_feats.shape
    emb = head.shape[1]
    negatives = neg_ids.shape[1]
    n_dp = lax.axis_size("dp")
    n_group = lax.axis_size("group")
    block = width // (n_dp * n_group)
    me_g = lax.axis_index("group")

    feats = jnp.stack([query_feats, passage_feats]).reshape(2, rows, n_dp, n_group, block)
    feats = feats.transpose(3, 0, 1, 2, 4).reshape(n_group, 2 * rows, n_dp * block)
    feats = lax.all_to_all(feats, "group", split_axis=0, concat_axis=0, tiled=True)
    feats = feats.reshape(n_group * 2 * rows, n_dp * block)

    proj_query = jnp.dot(query_feats, head, preferred_element_type=jnp.float32).astype(jnp.bfloat16)
    proj_pass = jnp.dot(passage_feats, head, preferred_element_type=jnp.float32).astype(
        jnp.bfloat16
    )
    col_high = jnp.maximum(jnp.max(proj_query, axis=0), jnp.max(proj_pass, axis=0)).astype(
        jnp.float32
    )
    col_low = jnp.minimum(jnp.min(proj_query, axis=0), jnp.min(proj_pass, axis=0)).astype(
        jnp.float32
    )
    bounds = all_bounds(jnp.stack([col_high, -col_low]), n_dp, n_group)
    high_bound, low_bound = bounds[0], -bounds[1]

    query, quant_query, inv_query = quantize(proj_query, low_bound, high_bound)
    passage, quant_pass, inv_pass = quantize(proj_pass, low_bound, high_bound)
    batch_pass = lax.all_gather(passage, "group", axis=0, tiled=True)
    dp_pass = lax.all_gather(passage, "dp", axis=0, tiled=True)
    batch_query = lax.all_gather(query, "group", axis=0, tiled=True)
    dp_query = lax.all_gather(query, "dp", axis=0, tiled=True)

    named = (neg_ids // (n_group * rows)) * rows + neg_ids % rows
    places = jnp.arange(n_dp * rows, dtype=jnp.int32)[None, :]
    is_hard = named[:, 0:1] == places
    for k in range(1, negatives):
        is_hard = is_hard | (named[:, k : k + 1] == places)

    pos_mask = (
        jnp.arange(n_group * rows)[None, :] == (me_g * rows + jnp.arange(rows))[:, None]
    ).astype(jnp.float32)
    scores = dot_nt(query, batch_pass) / scaling_divisor
    hard_scores = dot_nt(query, dp_pass) / scaling_divisor
    positive = jnp.sum(scores * pos_mask, axis=1)
    exp_batch = jnp.exp(scores)
    batch_total = jnp.sum(exp_batch, axis=1)
    exp_pos = jnp.exp(positive)
    hard_exp = jnp.where(is_hard, jnp.exp(hard_scores), 0.0)
    hard_total = exp_pos + jnp.sum(hard_exp, axis=1)
    query_loss = jnp.log(batch_total) - positive + jnp.log(hard_total) - positive
    batch_weight = (
        exp_batch / batch_total[:, None] - pos_mask * (2.0 - exp_pos / hard_total)[:, None]
    ).astype(jnp.bfloat16)
    hard_weight = (hard_exp / hard_total[:, None]).astype(jnp.bfloat16)

    batch_arrived = lax.all_to_all(batch_weight, "group", split_axis=1, concat_axis=0, tiled=True)
    hard_arrived = lax.all_to_all(hard_weight, "dp", split_axis=1, concat_axis=0, tiled=True)

    query_grad = (
        jnp.dot(batch_weight, batch_pass, preferred_element_type=jnp.float32)
        + jnp.dot(hard_weight, dp_pass, preferred_element_type=jnp.float32)
    ) / scaling_divisor
    dy_query = norm_back(query_grad, quant_query, inv_query)

    one_weight = jnp.sum(hard_arrived.astype(jnp.float32), axis=1, keepdims=True)
    hard_grad = (one_weight * dp_query.astype(jnp.float32) / scaling_divisor).astype(jnp.bfloat16)
    chosen = (hard_arrived != 0).astype(jnp.bfloat16)
    pass_grad = dot_tn(batch_arrived, batch_query) / scaling_divisor + dot_tn(chosen, hard_grad)
    dy_pass = norm_back(pass_grad, quant_pass, inv_pass)

    dy = lax.all_gather(jnp.concatenate([dy_query, dy_pass]), "group", axis=0, tiled=True)
    partial = dot_tn(feats, dy).astype(jnp.bfloat16).reshape(n_dp, block, emb)
    shares = lax.all_to_all(partial, "dp", split_axis=0, concat_axis=0, tiled=True)
    head_grad = jnp.sum(shares.astype(jnp.float32), axis=0)
    return (head_grad, query_loss)


def solution(mesh):
    return jax.shard_map(
        body,
        mesh=mesh,
        in_specs=(
            P(("dp", "group"), None),
            P(("dp", "group"), None),
            P(),
            P(("dp", "group"), None),
        ),
        out_specs=(P(("dp", "group"), None), P(("dp", "group"))),
        check_vma=False,
    )
```

```python
import functools

import jax
import jax.numpy as jnp
from jax import lax
from jax.experimental import pallas as pl
from jax.experimental.pallas import tpu as pltpu
from jax.sharding import PartitionSpec as P

scaling_divisor = 0.05
levels = 15.0
epsilon = 1e-06
MESH = pl.DeviceIdType.MESH
VMEM = pl.BlockSpec(memory_space=pltpu.VMEM)


def quantize(projected, low_bound, high_bound):
    as_float = projected.astype(jnp.float32)
    step_size = (high_bound - low_bound) / levels
    level_pos = (as_float - low_bound) / step_size
    quantized = low_bound + step_size * (
        level_pos - jnp.sin(2.0 * jnp.pi * level_pos) / (2.0 * jnp.pi)
    )
    inverse = lax.rsqrt(jnp.sum(quantized * quantized, axis=-1, keepdims=True) + epsilon)
    return ((quantized * inverse).astype(jnp.bfloat16), quantized, inverse)


def norm_back(cotangent, quantized, inverse):
    inner_prod = jnp.sum(quantized * cotangent, axis=-1, keepdims=True)
    return (inverse * cotangent - quantized * inverse**3 * inner_prod).astype(jnp.bfloat16)


def bounds_kernel(n_dp, n_group, own, out, from_group, from_dp, mid, send_g, recv_g, send_d, recv_d):
    me_d, me_g = lax.axis_index("dp"), lax.axis_index("group")

    def exchange(src, landing, send, recv, count, target):
        copies = []
        for k in range(1, count):
            copy = pltpu.make_async_remote_copy(
                src_ref=src,
                dst_ref=landing.at[k],
                send_sem=send.at[k],
                recv_sem=recv.at[k],
                device_id=target(k),
                device_id_type=MESH,
            )
            copy.start()
            copies.append(copy)
        for copy in copies:
            copy.wait()
        total = src[...]
        for k in range(1, count):
            total = jnp.maximum(total, landing[k])
        return total

    mid[...] = exchange(
        own, from_group, send_g, recv_g, n_group, lambda k: (me_d, lax.rem(me_g + k, n_group))
    )
    out[...] = exchange(
        mid, from_dp, send_d, recv_d, n_dp, lambda k: (lax.rem(me_d + k, n_dp), me_g)
    )


def all_bounds(own, n_dp, n_group):
    return pl.pallas_call(
        functools.partial(bounds_kernel, n_dp, n_group),
        out_shape=jax.ShapeDtypeStruct(own.shape, own.dtype),
        in_specs=[VMEM],
        out_specs=VMEM,
        scratch_shapes=[
            pltpu.VMEM((n_group,) + own.shape, own.dtype),
            pltpu.VMEM((n_dp,) + own.shape, own.dtype),
            pltpu.VMEM(own.shape, own.dtype),
            pltpu.SemaphoreType.DMA((n_group,)),
            pltpu.SemaphoreType.DMA((n_group,)),
            pltpu.SemaphoreType.DMA((n_dp,)),
            pltpu.SemaphoreType.DMA((n_dp,)),
        ],
        compiler_params=pltpu.CompilerParams(has_side_effects=True),
        name="bounds",
    )(own)


def remote(src, dst, send, recv, device):
    return pltpu.make_async_remote_copy(
        src_ref=src,
        dst_ref=dst,
        send_sem=send,
        recv_sem=recv,
        device_id=device,
        device_id_type=MESH,
    )


def gather_kernel(
    n_dp, n_group, inner, passage, query, feats,
    batch_pass, dp_pass, batch_query, dp_query, feats_out,
    send_line, send_pair, recv_dp, send_group, recv_group, local_sem,
):
    me_d, me_g = lax.axis_index("dp"), lax.axis_index("group")
    line = n_dp // inner
    z, y = me_d // inner, lax.rem(me_d, inner)
    items = ((passage, batch_pass, dp_pass), (query, batch_query, dp_query))

    def slot_copy(i, source, src, send, target):
        return remote(src, items[i][2].at[source], send, recv_dp.at[i, source], (target, me_g))

    def forwards(i, at, src, rightward, leftward):
        source = at * inner + y
        copies = []
        if rightward:
            copies.append(
                (z < line - 1, slot_copy(i, source, src, send_line.at[i, 0, at], lax.rem(me_d + inner, n_dp)))
            )
        if leftward:
            copies.append(
                (z > 0, slot_copy(i, source, src, send_line.at[i, 1, at], lax.rem(me_d + n_dp - inner, n_dp)))
            )
        for k in range(1, inner):
            target = z * inner + lax.rem(y + k, inner)
            copies.append((None, slot_copy(i, source, src, send_pair.at[i, k, at], target)))
        return copies

    def each(copies, act):
        for condition, copy in copies:
            if condition is None:
                act(copy)
            else:
                pl.when(condition)(functools.partial(act, copy))

    def start(copy):
        copy.start()

    def wait_send(copy):
        copy.wait_send()

    def group_copy(j, src, dst, k):
        target = lax.rem(me_g + k, n_group)
        return remote(
            src(target), dst.at[me_g], send_group.at[j, k], recv_group.at[j, k], (me_d, target)
        )

    def group_copies(j, k):
        if j < 2:
            return group_copy(j, lambda target: items[j][0], items[j][1], k)
        return group_copy(j, lambda target: feats.at[target], feats_out, k)

    for i in range(2):
        each(forwards(i, z, items[i][0], True, True), start)
        for k in range(1, n_group):
            group_copies(i, k).start()
    for k in range(1, n_group):
        group_copies(2, k).start()
    local = []
    for i, (own, batch, over_dp) in enumerate(items):
        local.append(pltpu.make_async_copy(own, batch.at[me_g], local_sem.at[2 * i]))
        local.append(pltpu.make_async_copy(own, over_dp.at[me_d], local_sem.at[2 * i + 1]))
    local.append(pltpu.make_async_copy(feats.at[me_g], feats_out.at[me_g], local_sem.at[4]))
    for copy in local:
        copy.start()

    for s in range(1, line):
        for i in range(2):
            for at, inside, onward in ((z - s, z >= s, True), (z + s, z + s < line, False)):

                @pl.when(inside)
                def _(i=i, at=at, onward=onward):
                    source = at * inner + y
                    block = items[i][2].at[source]
                    slot_copy(i, source, block, send_line.at[i, 0, at], me_d).wait_recv()
                    each(forwards(i, at, block, onward, not onward), start)

    for i in range(2):
        for k in range(1, inner):
            for at in range(line):
                source = at * inner + lax.rem(y + k, inner)
                block = items[i][2].at[source]
                slot_copy(i, source, block, send_pair.at[i, k, at], me_d).wait_recv()
        each(forwards(i, z, items[i][0], True, True), wait_send)
    for s in range(1, line):
        for i in range(2):
            for at, inside, onward in ((z - s, z >= s, True), (z + s, z + s < line, False)):

                @pl.when(inside)
                def _(i=i, at=at, onward=onward):
                    block = items[i][2].at[at * inner + y]
                    each(forwards(i, at, block, onward, not onward), wait_send)

    for j in range(3):
        for k in range(1, n_group):
            group_copies(j, k).wait_send()
            dst = (batch_pass, batch_query, feats_out)[j]
            landed = dst.at[lax.rem(me_g + n_group - k, n_group)]
            remote(
                landed, landed, send_group.at[j, k], recv_group.at[j, k], (me_d, me_g)
            ).wait_recv()
    for copy in local:
        copy.wait()


def gather_all(passage, query, feats, n_dp, n_group):
    inner = 2 if n_dp % 2 == 0 else 1
    line = n_dp // inner
    dtype = passage.dtype
    over = lambda n: jax.ShapeDtypeStruct((n,) + passage.shape, dtype)
    anywhere = pl.BlockSpec(memory_space=pl.ANY)
    return pl.pallas_call(
        functools.partial(gather_kernel, n_dp, n_group, inner),
        out_shape=(
            over(n_group), over(n_dp), over(n_group), over(n_dp),
            jax.ShapeDtypeStruct(feats.shape, dtype),
        ),
        in_specs=[VMEM] * 3,
        out_specs=(anywhere,) * 5,
        scratch_shapes=[
            pltpu.SemaphoreType.DMA((2, 2, line)),
            pltpu.SemaphoreType.DMA((2, inner, line)),
            pltpu.SemaphoreType.DMA((2, n_dp)),
            pltpu.SemaphoreType.DMA((3, n_group)),
            pltpu.SemaphoreType.DMA((3, n_group)),
            pltpu.SemaphoreType.DMA((5,)),
        ],
        compiler_params=pltpu.CompilerParams(has_side_effects=True),
        name="gather",
    )(passage, query, feats)


def reduce_kernel(
    n_dp, n_group, inner, chunks, dy, feats, out,
    turned, gathered, total, pair_out, pair_in, line_out, line_in, kept,
    send_g, recv_g, send_p, recv_p, send_l, recv_l,
):
    me_d, me_g = lax.axis_index("dp"), lax.axis_index("group")
    line = n_dp // inner
    z, y = me_d // inner, lax.rem(me_d, inner)
    tokens, emb = dy.shape
    wide = emb // chunks
    block = out.shape[0]
    columns = lambda c: pl.ds(c * wide, wide)

    def dy_copy(c, k):
        target = lax.rem(me_g + k, n_group)
        return remote(
            dy.at[:, columns(c)], gathered.at[k, :, columns(c)],
            send_g.at[c, k], recv_g.at[c, k], (me_d, target),
        )

    def pair_copy(c, k):
        target = z * inner + lax.rem(y + k, inner)
        return remote(
            pair_out.at[c, k], pair_in.at[c, k], send_p.at[c, k], recv_p.at[c, k], (target, me_g)
        )

    def line_copy(c, j):
        target = lax.rem(z + j, line) * inner + y
        return remote(
            line_out.at[c, j], line_in.at[c, j], send_l.at[c, j], recv_l.at[c, j], (target, me_g)
        )

    for c in range(chunks):
        for k in range(1, n_group):
            dy_copy(c, k).start()
    for k in range(n_group):
        turned[k] = feats[lax.rem(me_g + n_group - k, n_group)].T

    def first(c):
        part = jnp.dot(turned[0], dy[:, columns(c)], preferred_element_type=jnp.float32)
        for k in range(1, n_group):
            dy_copy(c, k).wait()
            part += jnp.dot(
                turned[k], gathered[k, :, columns(c)], preferred_element_type=jnp.float32
            )
        total[c] = part.reshape(n_dp, block, wide)
        for k in range(1, inner):
            for at in range(line):
                pair_out[c, k, at] = total[c, at * inner + lax.rem(y + k, inner)].astype(
                    jnp.bfloat16
                )
            pair_copy(c, k).start()

    def second(c):
        for k in range(1, inner):
            pair_copy(c, k).wait()

        def summed(at):
            value = total[c, at * inner + y]
            for k in range(1, inner):
                value += pair_in[c, k, at].astype(jnp.float32)
            return value

        for j in range(1, line):
            line_out[c, j] = summed(lax.rem(z + j, line)).astype(jnp.bfloat16)
            line_copy(c, j).start()
        kept[c] = summed(z)

    def third(c):
        value = kept[c]
        for j in range(1, line):
            line_copy(c, j).wait()
            value += line_in[c, j].astype(jnp.float32)
        out[:, columns(c)] = value

    for c in range(chunks):
        first(c)
        if c:
            second(c - 1)
    second(chunks - 1)
    for c in range(chunks):
        third(c)


def reduce_head(dy, feats, n_dp, n_group, block):
    inner = 2 if n_dp % 2 == 0 else 1
    line = n_dp // inner
    tokens, emb = dy.shape
    depth = feats.shape[2]
    chunks = max(1, emb // 256)
    wide = emb // chunks
    bf16 = lambda *shape: pltpu.VMEM(shape, jnp.bfloat16)
    f32 = lambda *shape: pltpu.VMEM(shape, jnp.float32)
    sems = lambda *shape: pltpu.SemaphoreType.DMA(shape)
    return pl.pallas_call(
        functools.partial(reduce_kernel, n_dp, n_group, inner, chunks),
        out_shape=jax.ShapeDtypeStruct((block, emb), jnp.float32),
        in_specs=[VMEM] * 2,
        out_specs=VMEM,
        scratch_shapes=[
            bf16(n_group, depth, tokens),
            bf16(n_group, tokens, emb),
            f32(chunks, n_dp, block, wide),
            bf16(chunks, inner, line, block, wide),
            bf16(chunks, inner, line, block, wide),
            bf16(chunks, line, block, wide),
            bf16(chunks, line, block, wide),
            f32(chunks, block, wide),
            sems(chunks, n_group), sems(chunks, n_group),
            sems(chunks, inner), sems(chunks, inner),
            sems(chunks, line), sems(chunks, line),
        ],
        compiler_params=pltpu.CompilerParams(has_side_effects=True),
        name="reduce",
    )(dy, feats)


def dot_nt(a, b):
    return lax.dot_general(a, b, (((1,), (1,)), ((), ())), preferred_element_type=jnp.float32)


def dot_tn(a, b):
    return lax.dot_general(a, b, (((0,), (0,)), ((), ())), preferred_element_type=jnp.float32)


def body(query_feats, passage_feats, head, neg_ids):
    rows, width = query_feats.shape
    emb = head.shape[1]
    negatives = neg_ids.shape[1]
    n_dp = lax.axis_size("dp")
    n_group = lax.axis_size("group")
    block = width // (n_dp * n_group)
    me_g = lax.axis_index("group")

    feats = jnp.stack([query_feats, passage_feats]).reshape(2, rows, n_dp, n_group, block)
    feats = feats.transpose(3, 0, 1, 2, 4).reshape(n_group, 2 * rows, n_dp * block)

    proj_query = jnp.dot(query_feats, head, preferred_element_type=jnp.float32).astype(jnp.bfloat16)
    proj_pass = jnp.dot(passage_feats, head, preferred_element_type=jnp.float32).astype(
        jnp.bfloat16
    )
    col_high = jnp.maximum(jnp.max(proj_query, axis=0), jnp.max(proj_pass, axis=0)).astype(
        jnp.float32
    )
    col_low = jnp.minimum(jnp.min(proj_query, axis=0), jnp.min(proj_pass, axis=0)).astype(
        jnp.float32
    )
    bounds = all_bounds(jnp.stack([col_high, -col_low]), n_dp, n_group)
    high_bound, low_bound = bounds[0], -bounds[1]

    query, quant_query, inv_query = quantize(proj_query, low_bound, high_bound)
    passage, quant_pass, inv_pass = quantize(proj_pass, low_bound, high_bound)
    batch_pass, dp_pass, batch_query, dp_query, feats = gather_all(
        passage, query, feats, n_dp, n_group
    )
    batch_pass, dp_pass, batch_query, dp_query = (
        x.reshape(-1, emb) for x in (batch_pass, dp_pass, batch_query, dp_query)
    )

    named = (neg_ids // (n_group * rows)) * rows + neg_ids % rows
    places = jnp.arange(n_dp * rows, dtype=jnp.int32)[None, :]
    is_hard = named[:, 0:1] == places
    for k in range(1, negatives):
        is_hard = is_hard | (named[:, k : k + 1] == places)

    pos_mask = (
        jnp.arange(n_group * rows)[None, :] == (me_g * rows + jnp.arange(rows))[:, None]
    ).astype(jnp.float32)
    scores = dot_nt(query, batch_pass) / scaling_divisor
    hard_scores = dot_nt(query, dp_pass) / scaling_divisor
    positive = jnp.sum(scores * pos_mask, axis=1)
    exp_batch = jnp.exp(scores)
    batch_total = jnp.sum(exp_batch, axis=1)
    exp_pos = jnp.exp(positive)
    hard_exp = jnp.where(is_hard, jnp.exp(hard_scores), 0.0)
    hard_total = exp_pos + jnp.sum(hard_exp, axis=1)
    query_loss = jnp.log(batch_total) - positive + jnp.log(hard_total) - positive
    batch_weight = (
        exp_batch / batch_total[:, None] - pos_mask * (2.0 - exp_pos / hard_total)[:, None]
    ).astype(jnp.bfloat16)
    hard_weight = (hard_exp / hard_total[:, None]).astype(jnp.bfloat16)

    batch_arrived = lax.all_to_all(batch_weight, "group", split_axis=1, concat_axis=0, tiled=True)
    hard_arrived = lax.all_to_all(hard_weight, "dp", split_axis=1, concat_axis=0, tiled=True)

    query_grad = (
        jnp.dot(batch_weight, batch_pass, preferred_element_type=jnp.float32)
        + jnp.dot(hard_weight, dp_pass, preferred_element_type=jnp.float32)
    ) / scaling_divisor
    dy_query = norm_back(query_grad, quant_query, inv_query)

    one_weight = jnp.sum(hard_arrived.astype(jnp.float32), axis=1, keepdims=True)
    hard_grad = (one_weight * dp_query.astype(jnp.float32) / scaling_divisor).astype(jnp.bfloat16)
    chosen = (hard_arrived != 0).astype(jnp.bfloat16)
    pass_grad = dot_tn(batch_arrived, batch_query) / scaling_divisor + dot_tn(chosen, hard_grad)
    dy_pass = norm_back(pass_grad, quant_pass, inv_pass)

    dy = jnp.concatenate([dy_query, dy_pass])
    head_grad = reduce_head(dy, feats, n_dp, n_group, block)
    return (head_grad, query_loss)


def solution(mesh):
    return jax.shard_map(
        body,
        mesh=mesh,
        in_specs=(
            P(("dp", "group"), None),
            P(("dp", "group"), None),
            P(),
            P(("dp", "group"), None),
        ),
        out_specs=(P(("dp", "group"), None), P(("dp", "group"))),
        check_vma=False,
    )
```

```python
import functools
import math

import jax
import jax.numpy as jnp
from jax import lax
from jax.experimental import pallas as pl
from jax.experimental.pallas import tpu as pltpu
from jax.sharding import PartitionSpec as P

scaling_divisor = 0.05
levels = 15.0
epsilon = 1e-06
MESH = pl.DeviceIdType.MESH
VMEM = pl.BlockSpec(memory_space=pltpu.VMEM)


def quantize(projected, low, stride, inv_stride):
    level = (projected.astype(jnp.float32) - low) * inv_stride
    turn = level - jnp.floor(level + 0.5)
    quarter = 0.25 - jnp.abs(jnp.abs(turn) - 0.25)
    angle = jnp.where(turn < 0, -quarter, quarter) * (2.0 * math.pi)
    square = angle * angle
    series = -1.0 / math.factorial(11)
    for order in (9, 7, 5, 3, 1):
        series = (-1.0) ** (order // 2) / math.factorial(order) + square * series
    return low + stride * (level - angle * series * (1.0 / (2.0 * math.pi)))


def norm_back(cotangent, quantized, inverse):
    inner_prod = jnp.sum(quantized * cotangent, axis=-1, keepdims=True)
    return (inverse * cotangent - quantized * (inverse**3 * inner_prod)).astype(jnp.bfloat16)


def dot_nn(a, b):
    return jnp.dot(a, b, preferred_element_type=jnp.float32)


def dot_nt(a, b):
    return lax.dot_general(a, b, (((1,), (1,)), ((), ())), preferred_element_type=jnp.float32)


def dot_tn(a, b):
    return lax.dot_general(a, b, (((0,), (0,)), ((), ())), preferred_element_type=jnp.float32)


def remote(src, dst, send, recv, device):
    return pltpu.make_async_remote_copy(
        src_ref=src,
        dst_ref=dst,
        send_sem=send,
        recv_sem=recv,
        device_id=device,
        device_id_type=MESH,
    )


def step_kernel(
    n_dp, n_group, inner, chunks,
    proj_query, proj_pass, stats, query_feats, pass_feats, named, out, loss,
    stats_group, stats_dp, stats_mid,
    emb_query, emb_pass, quant_query, quant_pass, inv_query, inv_pass,
    batch_query, batch_pass, dp_query, dp_pass, hard_exp,
    batch_out, batch_in, hard_out, hard_in,
    feats, turned, dy, gathered, total, pair_out, pair_in, line_out, line_in, kept,
    s_stat_g, r_stat_g, s_stat_d, r_stat_d, s_feat, r_feat,
    s_line, s_pair, r_dp, s_batch, r_batch, s_bw, r_bw, s_hw, r_hw,
    s_dy, r_dy, s_p, r_p, s_l, r_l,
):
    me_d, me_g = lax.axis_index("dp"), lax.axis_index("group")
    line = n_dp // inner
    z, y = me_d // inner, lax.rem(me_d, inner)
    rows, emb = proj_query.shape
    wide = emb // chunks
    block = out.shape[0]
    columns = lambda c: pl.ds(c * wide, wide)
    group_at = lambda k: lax.rem(me_g + k, n_group)
    group_from = lambda k: lax.rem(me_g + n_group - k, n_group)
    dp_at = lambda k: lax.rem(me_d + k, n_dp)
    dp_from = lambda k: lax.rem(me_d + n_dp - k, n_dp)

    def feat_copy(i, k):
        src = (query_feats, pass_feats)[i]
        return remote(
            src.at[group_at(k)], feats.at[i, k], s_feat.at[i, k], r_feat.at[i, k], (me_d, group_at(k))
        )

    def largest(src, landing, send, recv, count, target):
        copies = []
        for k in range(1, count):
            copies.append(remote(src, landing.at[k], send.at[k], recv.at[k], target(k)))
            copies[-1].start()
        value = src[...]
        for k in range(1, count):
            copies[k - 1].wait()
            value = jnp.maximum(value, landing[k])
        return value

    stats_mid[...] = largest(
        stats, stats_group, s_stat_g, r_stat_g, n_group, lambda k: (me_d, group_at(k))
    )
    for i in range(2):
        for k in range(1, n_group):
            feat_copy(i, k).start()
    bounds = largest(stats_mid, stats_dp, s_stat_d, r_stat_d, n_dp, lambda k: (dp_at(k), me_g))
    high, low = bounds[0:1], -bounds[1:2]
    stride = (high - low) / levels
    inv_stride = 1.0 / stride

    items = ((emb_pass, batch_pass, dp_pass), (emb_query, batch_query, dp_query))

    def slot_copy(i, source, src, send, target):
        return remote(src, items[i][2].at[source], send, r_dp.at[i, source], (target, me_g))

    def forwards(i, at, src, rightward, leftward):
        source = at * inner + y
        copies = []
        if rightward:
            copies.append((z < line - 1, slot_copy(i, source, src, s_line.at[i, 0, at], dp_at(inner))))
        if leftward:
            copies.append((z > 0, slot_copy(i, source, src, s_line.at[i, 1, at], dp_from(inner))))
        for k in range(1, inner):
            target = z * inner + lax.rem(y + k, inner)
            copies.append((None, slot_copy(i, source, src, s_pair.at[i, k, at], target)))
        return copies

    def each(copies, act):
        for condition, copy in copies:
            if condition is None:
                act(copy)
            else:
                pl.when(condition)(functools.partial(act, copy))

    def start(copy):
        copy.start()

    def wait_send(copy):
        copy.wait_send()

    def batch_copy(i, k):
        return remote(
            items[i][0], items[i][1].at[k], s_batch.at[i, k], r_batch.at[i, k], (me_d, group_at(k))
        )

    def start_own(i):
        each(forwards(i, z, items[i][0], True, True), start)
        for k in range(1, n_group):
            batch_copy(i, k).start()

    def relay(i, s):
        for at, inside, onward in ((z - s, z >= s, True), (z + s, z + s < line, False)):

            @pl.when(inside)
            def _(at=at, onward=onward):
                source = at * inner + y
                arrived = items[i][2].at[source]
                slot_copy(i, source, arrived, s_line.at[i, 0, at], me_d).wait_recv()
                each(forwards(i, at, arrived, onward, not onward), start)

    def wait_pairs(i):
        for k in range(1, inner):
            for at in range(line):
                source = at * inner + lax.rem(y + k, inner)
                arrived = items[i][2].at[source]
                slot_copy(i, source, arrived, s_pair.at[i, k, at], me_d).wait_recv()

    def wait_all_sent(i):
        each(forwards(i, z, items[i][0], True, True), wait_send)
        for s in range(1, line):
            for at, inside, onward in ((z - s, z >= s, True), (z + s, z + s < line, False)):

                @pl.when(inside)
                def _(at=at, onward=onward):
                    arrived = items[i][2].at[at * inner + y]
                    each(forwards(i, at, arrived, onward, not onward), wait_send)

    def embed(projected, quant, inverse, emb_ref):
        value = quantize(projected[...], low, stride, inv_stride)
        inv = lax.rsqrt(jnp.sum(value * value, axis=-1, keepdims=True) + epsilon)
        quant[...] = value
        inverse[...] = inv
        emb_ref[...] = (value * inv).astype(jnp.bfloat16)

    embed(proj_pass, quant_pass, inv_pass, emb_pass)
    start_own(0)
    embed(proj_query, quant_query, inv_query, emb_query)
    for s in range(1, line):
        relay(0, s)
    start_own(1)

    for i in range(2):
        for k in range(1, n_group):
            feat_copy(i, k).wait()
        lanes = pl.ds(i * rows, rows)
        turned[0, :, lanes] = (query_feats, pass_feats)[i][me_g].T
        for k in range(1, n_group):
            turned[k, :, lanes] = feats[i, k].T

    for k in range(1, n_group):
        batch_copy(0, k).wait()
    wait_pairs(0)
    if line > 1:
        relay(1, 1)

    def over_dp(step, value):
        if n_dp > 16:
            return lax.fori_loop(1, n_dp, step, value)
        for k in range(1, n_dp):
            value = step(k, value)
        return value

    query = emb_query[...]
    eye = (
        lax.broadcasted_iota(jnp.int32, (rows, rows), 0)
        == lax.broadcasted_iota(jnp.int32, (rows, rows), 1)
    ).astype(jnp.float32)
    place = lax.broadcasted_iota(jnp.int32, (rows, rows), 1)
    batch_block = lambda k: emb_pass[...] if k == 0 else batch_pass[k]
    scores = [dot_nt(query, batch_block(k)) / scaling_divisor for k in range(n_group)]
    positive = jnp.sum(scores[0] * eye, axis=1, keepdims=True)
    exp_batch = [jnp.exp(score) for score in scores]
    batch_total = sum(jnp.sum(value, axis=1, keepdims=True) for value in exp_batch)
    exp_pos = jnp.exp(positive)

    def hard_step(k, hard_sum):
        source = dp_at(k)
        score = dot_nt(query, dp_pass[source]) / scaling_divisor
        here = named[:, 0:1] == place + source * rows
        for n in range(1, named.shape[1]):
            here = here | (named[:, n : n + 1] == place + source * rows)
        value = jnp.where(here, jnp.exp(score), 0.0)
        hard_exp[k] = value
        return hard_sum + value

    hard_sum = over_dp(hard_step, jnp.zeros((rows, rows), jnp.float32))
    hard_total = exp_pos + jnp.sum(hard_sum, axis=1, keepdims=True)
    loss[...] = jnp.log(batch_total) - positive + jnp.log(hard_total) - positive

    def weight_copy(k):
        return remote(
            batch_out.at[k], batch_in.at[k], s_bw.at[k], r_bw.at[k], (me_d, group_from(k))
        )

    def hard_copy(k):
        return remote(hard_out.at[k], hard_in.at[k], s_hw.at[k], r_hw.at[k], (dp_at(k), me_g))

    for k in range(n_group):
        weight = exp_batch[k] / batch_total
        if k == 0:
            weight = weight - eye * (2.0 - exp_pos / hard_total)
        batch_out[k] = weight.astype(jnp.bfloat16)
        if k:
            weight_copy(k).start()

    def hard_send(k, nothing):
        hard_out[k] = (hard_exp[k] / hard_total).astype(jnp.bfloat16)
        hard_copy(k).start()
        return nothing

    over_dp(hard_send, 0)
    if line > 2:
        relay(1, 2)

    grad = dot_nn(batch_out[0], emb_pass[...])
    for k in range(1, n_group):
        grad += dot_nn(batch_out[k], batch_pass[k])
    grad = over_dp(lambda k, value: value + dot_nn(hard_out[k], dp_pass[dp_at(k)]), grad)
    dy[0] = norm_back(grad / scaling_divisor, quant_query[...], inv_query[...])

    def dy_copy(i, c, k):
        return remote(
            dy.at[i, :, columns(c)], gathered.at[k, pl.ds(i * rows, rows), columns(c)],
            s_dy.at[i, c, k], r_dy.at[i, c, k], (me_d, group_at(k)),
        )

    for c in range(chunks):
        for k in range(1, n_group):
            dy_copy(0, c, k).start()
    for s in range(3, line):
        relay(1, s)

    for k in range(1, n_group):
        batch_copy(1, k).wait()
        weight_copy(k).wait()
    grad = dot_tn(batch_out[0], emb_query[...])
    for k in range(1, n_group):
        grad += dot_tn(batch_in[k], batch_query[n_group - k])
    grad = grad / scaling_divisor
    wait_pairs(1)

    def hard_back(k, value):
        hard_copy(k).wait()
        weight = hard_in[k]
        one = jnp.sum(weight.astype(jnp.float32), axis=1, keepdims=True)
        hard = (one * dp_query[dp_from(k)].astype(jnp.float32) * (1.0 / scaling_divisor)).astype(
            jnp.bfloat16
        )
        chosen = jnp.where(weight.astype(jnp.float32) != 0, 1.0, 0.0).astype(jnp.bfloat16)
        return value + dot_tn(chosen, hard)

    dy[1] = norm_back(over_dp(hard_back, grad), quant_pass[...], inv_pass[...])
    for c in range(chunks):
        for k in range(1, n_group):
            dy_copy(1, c, k).start()

    def pair_copy(c, k):
        target = z * inner + lax.rem(y + k, inner)
        return remote(
            pair_out.at[c, k - 1], pair_in.at[c, k - 1], s_p.at[c, k], r_p.at[c, k], (target, me_g)
        )

    def line_copy(c, j):
        target = lax.rem(z + j, line) * inner + y
        return remote(
            line_out.at[c, j], line_in.at[c, j], s_l.at[c, j], r_l.at[c, j], (target, me_g)
        )

    def first(c):
        part = dot_nn(turned[0, :, 0:rows], dy[0, :, columns(c)])
        part += dot_nn(turned[0, :, rows:], dy[1, :, columns(c)])
        for k in range(1, n_group):
            dy_copy(0, c, k).wait()
            dy_copy(1, c, k).wait()
            part += dot_nn(turned[k], gathered[k, :, columns(c)])
        total[c] = part.reshape(n_dp, block, wide)
        for k in range(1, inner):
            for at in range(line):
                pair_out[c, k - 1, at] = total[c, at * inner + lax.rem(y + k, inner)].astype(
                    jnp.bfloat16
                )
            pair_copy(c, k).start()

    def second(c):
        for k in range(1, inner):
            pair_copy(c, k).wait()

        def summed(at):
            value = total[c, at * inner + y]
            for k in range(1, inner):
                value += pair_in[c, k - 1, at].astype(jnp.float32)
            return value

        for j in range(1, line):
            line_out[c, j] = summed(lax.rem(z + j, line)).astype(jnp.bfloat16)
            line_copy(c, j).start()
        kept[c] = summed(z)

    def third(c):
        value = kept[c]
        for j in range(1, line):
            line_copy(c, j).wait()
            value += line_in[c, j].astype(jnp.float32)
        out[:, columns(c)] = value

    for c in range(chunks):
        first(c)
        if c:
            second(c - 1)
    second(chunks - 1)
    for i in range(2):
        wait_all_sent(i)
    for c in range(chunks):
        third(c)


def whole_step(proj_query, proj_pass, stats, query_feats, pass_feats, named, n_dp, n_group, block):
    inner = 2 if n_dp % 2 == 0 else 1
    line = n_dp // inner
    rows, emb = proj_query.shape
    depth = query_feats.shape[2]
    chunks = max(1, emb // 256)
    wide = emb // chunks
    bf16 = lambda *shape: pltpu.VMEM(shape, jnp.bfloat16)
    f32 = lambda *shape: pltpu.VMEM(shape, jnp.float32)
    sems = lambda *shape: [pltpu.SemaphoreType.DMA(shape)]
    pairs = lambda *shape: sems(*shape) * 2
    return pl.pallas_call(
        functools.partial(step_kernel, n_dp, n_group, inner, chunks),
        out_shape=(
            jax.ShapeDtypeStruct((block, emb), jnp.float32),
            jax.ShapeDtypeStruct((rows, 1), jnp.float32),
        ),
        in_specs=[VMEM] * 6,
        out_specs=(VMEM, VMEM),
        scratch_shapes=[
            f32(n_group, 2, emb), f32(n_dp, 2, emb), f32(2, emb),
            bf16(rows, emb), bf16(rows, emb), f32(rows, emb), f32(rows, emb), f32(rows, 1), f32(rows, 1),
            bf16(n_group, rows, emb), bf16(n_group, rows, emb), bf16(n_dp, rows, emb), bf16(n_dp, rows, emb),
            f32(n_dp, rows, rows),
            bf16(n_group, rows, rows), bf16(n_group, rows, rows), bf16(n_dp, rows, rows), bf16(n_dp, rows, rows),
            bf16(2, n_group, rows, depth), bf16(n_group, depth, 2 * rows), bf16(2, rows, emb),
            bf16(n_group, 2 * rows, emb),
            f32(chunks, n_dp, block, wide),
            bf16(chunks, max(1, inner - 1), line, block, wide),
            bf16(chunks, max(1, inner - 1), line, block, wide),
            bf16(chunks, line, block, wide), bf16(chunks, line, block, wide),
            f32(chunks, block, wide),
        ]
        + pairs(n_group) + pairs(n_dp) + pairs(2, n_group)
        + sems(2, 2, line) + sems(2, inner, line) + sems(2, n_dp) + pairs(2, n_group)
        + pairs(n_group) + pairs(n_dp)
        + pairs(2, chunks, n_group) + pairs(chunks, inner) + pairs(chunks, line),
        compiler_params=pltpu.CompilerParams(has_side_effects=True, vmem_limit_bytes=67043328),
        name="step",
    )(proj_query, proj_pass, stats, query_feats, pass_feats, named)


def body(query_feats, passage_feats, head, neg_ids):
    rows, width = query_feats.shape
    emb = head.shape[1]
    n_dp = lax.axis_size("dp")
    n_group = lax.axis_size("group")
    block = width // (n_dp * n_group)

    def cut(feats):
        feats = feats.reshape(rows, n_dp, n_group, block)
        return feats.transpose(2, 0, 1, 3).reshape(n_group, rows, n_dp * block)

    proj_query = jnp.dot(query_feats, head, preferred_element_type=jnp.float32).astype(jnp.bfloat16)
    proj_pass = jnp.dot(passage_feats, head, preferred_element_type=jnp.float32).astype(
        jnp.bfloat16
    )
    col_high = jnp.maximum(jnp.max(proj_query, axis=0), jnp.max(proj_pass, axis=0)).astype(
        jnp.float32
    )
    col_low = jnp.minimum(jnp.min(proj_query, axis=0), jnp.min(proj_pass, axis=0)).astype(
        jnp.float32
    )
    named = (neg_ids // (n_group * rows)) * rows + neg_ids % rows
    head_grad, query_loss = whole_step(
        proj_query, proj_pass, jnp.stack([col_high, -col_low]), cut(query_feats),
        cut(passage_feats), named, n_dp, n_group, block,
    )
    return (head_grad, query_loss.reshape(rows))


def solution(mesh):
    return jax.shard_map(
        body,
        mesh=mesh,
        in_specs=(
            P(("dp", "group"), None),
            P(("dp", "group"), None),
            P(),
            P(("dp", "group"), None),
        ),
        out_specs=(P(("dp", "group"), None), P(("dp", "group"))),
        check_vma=False,
    )
```

```python
import functools
import math

import jax
import jax.numpy as jnp
from jax import lax
from jax.experimental import pallas as pl
from jax.experimental.pallas import tpu as pltpu
from jax.sharding import PartitionSpec as P

scaling_divisor = 0.05
levels = 15.0
epsilon = 1e-06
MESH = pl.DeviceIdType.MESH
VMEM = pl.BlockSpec(memory_space=pltpu.VMEM)


def quantize(projected, low, stride, inv_stride):
    level = (projected.astype(jnp.float32) - low) * inv_stride
    turn = level - jnp.floor(level + 0.5)
    quarter = 0.25 - jnp.abs(jnp.abs(turn) - 0.25)
    angle = jnp.where(turn < 0, -quarter, quarter) * (2.0 * math.pi)
    square = angle * angle
    series = -1.0 / math.factorial(11)
    for order in (9, 7, 5, 3, 1):
        series = (-1.0) ** (order // 2) / math.factorial(order) + square * series
    return low + stride * (level - angle * series * (1.0 / (2.0 * math.pi)))


def norm_back(cotangent, quantized, inverse):
    inner_prod = jnp.sum(quantized * cotangent, axis=-1, keepdims=True)
    return (inverse * cotangent - quantized * (inverse**3 * inner_prod)).astype(jnp.bfloat16)


def dot_nn(a, b):
    return jnp.dot(a, b, preferred_element_type=jnp.float32)


def dot_nt(a, b):
    return lax.dot_general(a, b, (((1,), (1,)), ((), ())), preferred_element_type=jnp.float32)


def dot_tn(a, b):
    return lax.dot_general(a, b, (((0,), (0,)), ((), ())), preferred_element_type=jnp.float32)


def remote(src, dst, send, recv, device):
    return pltpu.make_async_remote_copy(
        src_ref=src,
        dst_ref=dst,
        send_sem=send,
        recv_sem=recv,
        device_id=device,
        device_id_type=MESH,
    )


def step_kernel(
    n_dp, n_group, inner, chunks,
    proj_query, proj_pass, stats, query_feats, pass_feats, named, out, loss,
    stats_group, stats_dp, stats_mid,
    emb_query, emb_pass, quant_query, quant_pass, inv_query, inv_pass,
    batch_query, batch_pass, dp_query, dp_pass, hard_exp,
    batch_out, batch_in, hard_out, hard_in,
    feats, turned, dy, gathered, total, pair_out, pair_in, line_out, line_in, kept,
    s_stat_g, r_stat_g, s_stat_d, r_stat_d, s_feat, r_feat,
    s_line, s_pair, r_dp, s_batch, r_batch, s_bw, r_bw, s_hw, r_hw,
    s_dy, r_dy, s_p, r_p, s_l, r_l, *staged
):
    me_d, me_g = lax.axis_index("dp"), lax.axis_index("group")
    line = n_dp // inner
    z, y = me_d // inner, lax.rem(me_d, inner)
    rows, emb = proj_query.shape
    wide = emb // chunks
    block = out.shape[0]
    columns = lambda c: pl.ds(c * wide, wide)
    group_at = lambda k: lax.rem(me_g + k, n_group)
    group_from = lambda k: lax.rem(me_g + n_group - k, n_group)
    dp_at = lambda k: lax.rem(me_d + k, n_dp)
    dp_from = lambda k: lax.rem(me_d + n_dp - k, n_dp)

    cut_feats = (staged[0].at[0], staged[0].at[1]) if staged else (query_feats, pass_feats)

    def feat_copy(i, k):
        src = cut_feats[i]
        return remote(
            src.at[group_at(k)], feats.at[i, k], s_feat.at[i, k], r_feat.at[i, k], (me_d, group_at(k))
        )

    def largest(src, landing, send, recv, count, target):
        copies = []
        for k in range(1, count):
            copies.append(remote(src, landing.at[k], send.at[k], recv.at[k], target(k)))
            copies[-1].start()
        value = src[...]
        for k in range(1, count):
            copies[k - 1].wait()
            value = jnp.maximum(value, landing[k])
        return value

    if staged:
        for i, whole in enumerate((query_feats, pass_feats)):
            for d in range(n_dp):
                for g in range(n_group):
                    staged[0][i, g, :, d * block : (d + 1) * block] = whole[
                        :, (d * n_group + g) * block : (d * n_group + g + 1) * block
                    ]

    stats_mid[...] = largest(
        stats, stats_group, s_stat_g, r_stat_g, n_group, lambda k: (me_d, group_at(k))
    )
    for i in range(2):
        for k in range(1, n_group):
            feat_copy(i, k).start()
    bounds = largest(stats_mid, stats_dp, s_stat_d, r_stat_d, n_dp, lambda k: (dp_at(k), me_g))
    high, low = bounds[0:1], -bounds[1:2]
    stride = (high - low) / levels
    inv_stride = 1.0 / stride

    items = ((emb_pass, batch_pass, dp_pass), (emb_query, batch_query, dp_query))

    def slot_copy(i, source, src, send, target):
        return remote(src, items[i][2].at[source], send, r_dp.at[i, source], (target, me_g))

    def forwards(i, at, src, rightward, leftward):
        source = at * inner + y
        copies = []
        if rightward:
            copies.append((z < line - 1, slot_copy(i, source, src, s_line.at[i, 0, at], dp_at(inner))))
        if leftward:
            copies.append((z > 0, slot_copy(i, source, src, s_line.at[i, 1, at], dp_from(inner))))
        for k in range(1, inner):
            target = z * inner + lax.rem(y + k, inner)
            copies.append((None, slot_copy(i, source, src, s_pair.at[i, k, at], target)))
        return copies

    def each(copies, act):
        for condition, copy in copies:
            if condition is None:
                act(copy)
            else:
                pl.when(condition)(functools.partial(act, copy))

    def start(copy):
        copy.start()

    def wait_send(copy):
        copy.wait_send()

    def batch_copy(i, k):
        return remote(
            items[i][0], items[i][1].at[k], s_batch.at[i, k], r_batch.at[i, k], (me_d, group_at(k))
        )

    def start_own(i):
        each(forwards(i, z, items[i][0], True, True), start)
        for k in range(1, n_group):
            batch_copy(i, k).start()

    def relay(i, s):
        for at, inside, onward in ((z - s, z >= s, True), (z + s, z + s < line, False)):

            @pl.when(inside)
            def _(at=at, onward=onward):
                source = at * inner + y
                arrived = items[i][2].at[source]
                slot_copy(i, source, arrived, s_line.at[i, 0, at], me_d).wait_recv()
                each(forwards(i, at, arrived, onward, not onward), start)

    def wait_pairs(i):
        for k in range(1, inner):
            for at in range(line):
                source = at * inner + lax.rem(y + k, inner)
                arrived = items[i][2].at[source]
                slot_copy(i, source, arrived, s_pair.at[i, k, at], me_d).wait_recv()

    def wait_all_sent(i):
        each(forwards(i, z, items[i][0], True, True), wait_send)
        for s in range(1, line):
            for at, inside, onward in ((z - s, z >= s, True), (z + s, z + s < line, False)):

                @pl.when(inside)
                def _(at=at, onward=onward):
                    arrived = items[i][2].at[at * inner + y]
                    each(forwards(i, at, arrived, onward, not onward), wait_send)

    def embed(projected, quant, inverse, emb_ref):
        value = quantize(projected[...], low, stride, inv_stride)
        inv = lax.rsqrt(jnp.sum(value * value, axis=-1, keepdims=True) + epsilon)
        quant[...] = value
        inverse[...] = inv
        emb_ref[...] = (value * inv).astype(jnp.bfloat16)

    embed(proj_pass, quant_pass, inv_pass, emb_pass)
    start_own(0)
    embed(proj_query, quant_query, inv_query, emb_query)
    for s in range(1, line):
        relay(0, s)
    start_own(1)

    for i in range(2):
        for k in range(1, n_group):
            feat_copy(i, k).wait()
        lanes = pl.ds(i * rows, rows)
        turned[0, :, lanes] = cut_feats[i][me_g].T
        for k in range(1, n_group):
            turned[k, :, lanes] = feats[i, k].T

    for k in range(1, n_group):
        batch_copy(0, k).wait()
    wait_pairs(0)
    if line > 1:
        relay(1, 1)

    def over_dp(step, value):
        if n_dp > 16:
            return lax.fori_loop(1, n_dp, step, value)
        for k in range(1, n_dp):
            value = step(k, value)
        return value

    query = emb_query[...]
    eye = (
        lax.broadcasted_iota(jnp.int32, (rows, rows), 0)
        == lax.broadcasted_iota(jnp.int32, (rows, rows), 1)
    ).astype(jnp.float32)
    place = lax.broadcasted_iota(jnp.int32, (rows, rows), 1)
    batch_block = lambda k: emb_pass[...] if k == 0 else batch_pass[k]
    scores = [dot_nt(query, batch_block(k)) / scaling_divisor for k in range(n_group)]
    positive = jnp.sum(scores[0] * eye, axis=1, keepdims=True)
    exp_batch = [jnp.exp(score) for score in scores]
    batch_total = sum(jnp.sum(value, axis=1, keepdims=True) for value in exp_batch)
    exp_pos = jnp.exp(positive)

    def hard_step(k, hard_sum):
        source = dp_at(k)
        score = dot_nt(query, dp_pass[source]) / scaling_divisor
        here = named[:, 0:1] == place + source * rows
        for n in range(1, named.shape[1]):
            here = here | (named[:, n : n + 1] == place + source * rows)
        value = jnp.where(here, jnp.exp(score), 0.0)
        hard_exp[k] = value
        return hard_sum + value

    hard_sum = over_dp(hard_step, jnp.zeros((rows, rows), jnp.float32))
    hard_total = exp_pos + jnp.sum(hard_sum, axis=1, keepdims=True)
    column = jnp.log(batch_total) - positive + jnp.log(hard_total) - positive
    loss[...] = jnp.sum(column * eye, axis=0, keepdims=True)

    def weight_copy(k):
        return remote(
            batch_out.at[k], batch_in.at[k], s_bw.at[k], r_bw.at[k], (me_d, group_from(k))
        )

    def hard_copy(k):
        return remote(hard_out.at[k], hard_in.at[k], s_hw.at[k], r_hw.at[k], (dp_at(k), me_g))

    for k in range(n_group):
        weight = exp_batch[k] / batch_total
        if k == 0:
            weight = weight - eye * (2.0 - exp_pos / hard_total)
        batch_out[k] = weight.astype(jnp.bfloat16)
        if k:
            weight_copy(k).start()

    def hard_send(k, nothing):
        hard_out[k] = (hard_exp[k] / hard_total).astype(jnp.bfloat16)
        hard_copy(k).start()
        return nothing

    over_dp(hard_send, 0)
    if line > 2:
        relay(1, 2)

    grad = dot_nn(batch_out[0], emb_pass[...])
    for k in range(1, n_group):
        grad += dot_nn(batch_out[k], batch_pass[k])
    grad = over_dp(lambda k, value: value + dot_nn(hard_out[k], dp_pass[dp_at(k)]), grad)
    dy[0] = norm_back(grad / scaling_divisor, quant_query[...], inv_query[...])

    def dy_copy(i, c, k):
        return remote(
            dy.at[i, :, columns(c)], gathered.at[k, pl.ds(i * rows, rows), columns(c)],
            s_dy.at[i, c, k], r_dy.at[i, c, k], (me_d, group_at(k)),
        )

    for c in range(chunks):
        for k in range(1, n_group):
            dy_copy(0, c, k).start()
    for s in range(3, line):
        relay(1, s)

    for k in range(1, n_group):
        batch_copy(1, k).wait()
        weight_copy(k).wait()
    grad = dot_tn(batch_out[0], emb_query[...])
    for k in range(1, n_group):
        grad += dot_tn(batch_in[k], batch_query[n_group - k])
    grad = grad / scaling_divisor
    wait_pairs(1)

    def hard_back(k, value):
        hard_copy(k).wait()
        weight = hard_in[k]
        one = jnp.sum(weight.astype(jnp.float32), axis=1, keepdims=True)
        hard = (one * dp_query[dp_from(k)].astype(jnp.float32) * (1.0 / scaling_divisor)).astype(
            jnp.bfloat16
        )
        chosen = jnp.where(weight.astype(jnp.float32) != 0, 1.0, 0.0).astype(jnp.bfloat16)
        return value + dot_tn(chosen, hard)

    dy[1] = norm_back(over_dp(hard_back, grad), quant_pass[...], inv_pass[...])
    for c in range(chunks):
        for k in range(1, n_group):
            dy_copy(1, c, k).start()

    def pair_copy(c, k):
        target = z * inner + lax.rem(y + k, inner)
        return remote(
            pair_out.at[c, k - 1], pair_in.at[c, k - 1], s_p.at[c, k], r_p.at[c, k], (target, me_g)
        )

    def line_copy(c, j):
        target = lax.rem(z + j, line) * inner + y
        return remote(
            line_out.at[c, j], line_in.at[c, j], s_l.at[c, j], r_l.at[c, j], (target, me_g)
        )

    def first(c):
        part = dot_nn(turned[0, :, 0:rows], dy[0, :, columns(c)])
        part += dot_nn(turned[0, :, rows:], dy[1, :, columns(c)])
        for k in range(1, n_group):
            dy_copy(0, c, k).wait()
            dy_copy(1, c, k).wait()
            part += dot_nn(turned[k], gathered[k, :, columns(c)])
        total[c] = part.reshape(n_dp, block, wide)
        for k in range(1, inner):
            for at in range(line):
                pair_out[c, k - 1, at] = total[c, at * inner + lax.rem(y + k, inner)].astype(
                    jnp.bfloat16
                )
            pair_copy(c, k).start()

    def second(c):
        for k in range(1, inner):
            pair_copy(c, k).wait()

        def summed(at):
            value = total[c, at * inner + y]
            for k in range(1, inner):
                value += pair_in[c, k - 1, at].astype(jnp.float32)
            return value

        for j in range(1, line):
            line_out[c, j] = summed(lax.rem(z + j, line)).astype(jnp.bfloat16)
            line_copy(c, j).start()
        kept[c] = summed(z)

    def third(c):
        value = kept[c]
        for j in range(1, line):
            line_copy(c, j).wait()
            value += line_in[c, j].astype(jnp.float32)
        out[:, columns(c)] = value

    for c in range(chunks):
        first(c)
        if c:
            second(c - 1)
    second(chunks - 1)
    for i in range(2):
        wait_all_sent(i)
    for c in range(chunks):
        third(c)


def whole_step(proj_query, proj_pass, stats, query_feats, pass_feats, named, n_dp, n_group, block):
    inner = 2 if n_dp % 2 == 0 else 1
    line = n_dp // inner
    rows, emb = proj_query.shape
    depth = n_dp * block
    inside = query_feats.ndim == 2
    chunks = max(1, emb // 256)
    wide = emb // chunks
    bf16 = lambda *shape: pltpu.VMEM(shape, jnp.bfloat16)
    f32 = lambda *shape: pltpu.VMEM(shape, jnp.float32)
    sems = lambda *shape: [pltpu.SemaphoreType.DMA(shape)]
    pairs = lambda *shape: sems(*shape) * 2
    return pl.pallas_call(
        functools.partial(step_kernel, n_dp, n_group, inner, chunks),
        out_shape=(
            jax.ShapeDtypeStruct((block, emb), jnp.float32),
            jax.ShapeDtypeStruct((1, rows), jnp.float32),
        ),
        in_specs=[VMEM] * 6,
        out_specs=(VMEM, VMEM),
        scratch_shapes=[
            f32(n_group, 2, emb), f32(n_dp, 2, emb), f32(2, emb),
            bf16(rows, emb), bf16(rows, emb), f32(rows, emb), f32(rows, emb), f32(rows, 1), f32(rows, 1),
            bf16(n_group, rows, emb), bf16(n_group, rows, emb), bf16(n_dp, rows, emb), bf16(n_dp, rows, emb),
            f32(n_dp, rows, rows),
            bf16(n_group, rows, rows), bf16(n_group, rows, rows), bf16(n_dp, rows, rows), bf16(n_dp, rows, rows),
            bf16(2, n_group, rows, depth), bf16(n_group, depth, 2 * rows), bf16(2, rows, emb),
            bf16(n_group, 2 * rows, emb),
            f32(chunks, n_dp, block, wide),
            bf16(chunks, max(1, inner - 1), line, block, wide),
            bf16(chunks, max(1, inner - 1), line, block, wide),
            bf16(chunks, line, block, wide), bf16(chunks, line, block, wide),
            f32(chunks, block, wide),
        ]
        + pairs(n_group) + pairs(n_dp) + pairs(2, n_group)
        + sems(2, 2, line) + sems(2, inner, line) + sems(2, n_dp) + pairs(2, n_group)
        + pairs(n_group) + pairs(n_dp)
        + pairs(2, chunks, n_group) + pairs(chunks, inner) + pairs(chunks, line)
        + ([bf16(2, n_group, rows, depth)] if inside else []),
        compiler_params=pltpu.CompilerParams(has_side_effects=True, vmem_limit_bytes=67043328),
        name="step",
    )(proj_query, proj_pass, stats, query_feats, pass_feats, named)


def body(query_feats, passage_feats, head, neg_ids):
    rows, width = query_feats.shape
    emb = head.shape[1]
    n_dp = lax.axis_size("dp")
    n_group = lax.axis_size("group")
    block = width // (n_dp * n_group)

    def cut(feats):
        if block % 128 == 0:
            return feats
        feats = feats.reshape(rows, n_dp, n_group, block)
        return feats.transpose(2, 0, 1, 3).reshape(n_group, rows, n_dp * block)

    proj_query = jnp.dot(query_feats, head, preferred_element_type=jnp.float32).astype(jnp.bfloat16)
    proj_pass = jnp.dot(passage_feats, head, preferred_element_type=jnp.float32).astype(
        jnp.bfloat16
    )
    col_high = jnp.maximum(jnp.max(proj_query, axis=0), jnp.max(proj_pass, axis=0)).astype(
        jnp.float32
    )
    col_low = jnp.minimum(jnp.min(proj_query, axis=0), jnp.min(proj_pass, axis=0)).astype(
        jnp.float32
    )
    named = (neg_ids // (n_group * rows)) * rows + neg_ids % rows
    head_grad, query_loss = whole_step(
        proj_query, proj_pass, jnp.stack([col_high, -col_low]), cut(query_feats),
        cut(passage_feats), named, n_dp, n_group, block,
    )
    return (head_grad, query_loss.reshape(rows))


def solution(mesh):
    return jax.shard_map(
        body,
        mesh=mesh,
        in_specs=(
            P(("dp", "group"), None),
            P(("dp", "group"), None),
            P(),
            P(("dp", "group"), None),
        ),
        out_specs=(P(("dp", "group"), None), P(("dp", "group"))),
        check_vma=False,
    )
```
